256 devices in a mesh: aux: 8 (over z_lo, core), occ: 32 (over y, x, z_hi).
Axes of the slice: x: 4, y: 4, z: 8 (z_hi: 2, z_lo: 4; z = z_hi * 4 + z_lo), core: 2. Of those that a mesh axis runs over, the one named last changes fastest.
Arguments:
- factors: float32 [8192, 32, 512], P('aux', 'occ'), may hold values from -0.3 to 0.3
- eps_occ: float32 [32], P('occ'), may hold values from -2 to -0.3
- eps_virt: float32 [512], replicated, may hold values from 0.2 to 3
- pair_mask: int32 [32, 4], P('occ'), may hold values 0 or 1
Outputs:
- gradient: float32 [8192, 32, 512], P('aux', 'occ')
The draws below stay inside these ranges and needn't reach their ends.
Inputs may be any that keep to these rules, and one draw needn't show every extreme that they name: `pair_mask`: 1 marks a surviving pair.
All inputs are finite; a program needn't handle non-finite values. No bound on the sum of `pair_mask` on one device may be relied on, other than what follows from the above.
Results may differ from the reference program's by a relative error of at most 0.0003.
Values sent between devices are 32-bit elements; how exact they have to be, the bound alone decides.
A program may use at most 128 MiB of HBM per device.

```python
import jax
import jax.numpy as jnp
from jax import lax

VIRT = 512
OCC_DEV = 1
OFFSETS = 4
NAUX = 8192
NOCC = 32
N_OCC = 32


def place_ends(result, stream_key, least, largest):
    shape = result.shape
    place = [jax.random.randint(jax.random.fold_in(stream_key, axis), (), 0, shape[axis]) for axis in range(len(shape))]
    result = result.at[tuple(place)].set(least)
    longest = shape.index(max(shape))
    place[longest] = (place[longest] + 1) % shape[longest]
    return result.at[tuple(place)].set(largest)


def levels(rng, shape, shards, smallest, high):
    factor_of, own = 1.0, jax.random.fold_in(rng, 6)
    for axis_at, blocks in shards:
        steps = jnp.exp(jax.random.uniform(jax.random.fold_in(own, axis_at), (blocks,), jnp.float32, smallest / len(shards), high / len(shards)))
        factor_of = factor_of * jnp.repeat(steps, shape[axis_at] // blocks).reshape([-1 if axis == axis_at else 1 for axis in range(len(shape))])
    return factor_of


def scatter_about(stream_key, extent, deviation, bound, shards=(), kind=jnp.bfloat16):
    drawn = jax.random.normal(stream_key, extent, jnp.float32) * deviation
    if len(shards) > 0:
        drawn = levels(stream_key, extent, shards, -0.22, 0.18) * drawn
    return jnp.clip(drawn, min=-bound, max=bound).astype(kind)


def setup_inputs(seed: int = 0) -> dict:
    arg_keys = jax.random.split(jax.random.key(seed), 5)
    factors = scatter_about(arg_keys[0], (NAUX, NOCC, VIRT), 0.05, 0.3, ((0, 8), (1, 32)), jnp.float32)
    eps_occ = jnp.clip(-2.0 + 1.7 * jax.random.uniform(arg_keys[1], (NOCC,), jnp.float32) ** levels(arg_keys[1], (NOCC,), ((0, 32),), -0.2, 0.2), -2.0, -0.3)
    eps_virt = jnp.clip(jax.random.uniform(arg_keys[2], (VIRT,), jnp.float32, 0.2, 3.0), 0.2, 3.0)
    pair_mask = place_ends((jax.random.randint(arg_keys[3], (N_OCC, OFFSETS), 0, 4) < 3).astype(jnp.int32), jax.random.fold_in(arg_keys[3], 1), 0, 1)
    return {"factors": factors, "eps_occ": eps_occ, "eps_virt": eps_virt, "pair_mask": pair_mask}


def reference(factors, eps_occ, eps_virt, pair_mask):
    width = OCC_DEV * VIRT
    blocks = factors.reshape(NAUX, N_OCC, width)
    energies = (eps_virt[None, None, :] - eps_occ.reshape(N_OCC, OCC_DEV)[:, :, None]).reshape(N_OCC, width)

    def group(index):
        resident = lax.dynamic_index_in_dim(blocks, index, 1, keepdims=False)
        total = jnp.zeros((NAUX, width), jnp.float32)
        for offset in range(OFFSETS + 1):
            source = jnp.maximum(index - offset, 0).astype(jnp.int32)
            visitor = lax.dynamic_index_in_dim(blocks, source, 1, keepdims=False)
            if offset == 0:
                live = jnp.array(True)
            else:
                live = (index >= offset) & (pair_mask[index, offset - 1] > 0)
            integrals = lax.dot_general(resident, visitor, (((0,), (0,)), ((), ())), precision=lax.Precision.HIGHEST, preferred_element_type=jnp.float32)
            row_energy = lax.dynamic_index_in_dim(energies, index, 0, keepdims=False)
            col_energy = lax.dynamic_index_in_dim(energies, source, 0, keepdims=False)
            amplitude = -integrals / (row_energy[:, None] + col_energy[None, :])
            added = lax.dot_general(visitor, amplitude, (((1,), (1,)), ((), ())), precision=lax.Precision.HIGHEST, preferred_element_type=jnp.float32)
            total = total + jnp.where(live, added, jnp.zeros_like(added))
        return total

    stacked = lax.map(group, jnp.arange(N_OCC, dtype=jnp.int32))
    return stacked.transpose(1, 0, 2).reshape(NAUX, NOCC, VIRT)
```

```python
import jax
import jax.numpy as jnp
from jax import lax
from jax.experimental import pallas as pl
from jax.experimental.pallas import tpu as pltpu
from jax.sharding import PartitionSpec as P

OFFSETS = 4
LANES = 128
PAD = 8
MESH = pl.DeviceIdType.MESH
F32 = jnp.float32
BF16 = jnp.bfloat16

UNITS = [(0, 0, 1), (0, 1, 1), (0, 2, 1), (0, 3, 1), (2, 0, 1), (2, 1, 1), (2, 2, 1), (2, 3, 1), (4, 0, 1), (4, 1, 1), (4, 2, 1), (4, 3, 1), (1, 0, 1), (1, 1, 1), (1, 2, 1), (1, 3, 1), (3, 0, 1), (3, 1, 1), (3, 2, 1), (3, 3, 1)]
PLAN = [
    ([[], [], [], []], 'A3'),
    ([[], [], [], []], 'A0'),
    ([[], [], [], []], 'A1'),
    ([[], [], [], []], 'A2'),
    ([[], [], ['z0'], ['z0']], 'A4'),
    ([['v0'], ['v0'], ['v0', 'z1'], ['v0', 'z1']], 'A5'),
    ([['v1', 'v2', 'x0'], ['v1', 'v2', 'x0'], ['v1', 'x0'], ['v1', 'x0']], 'A12'),
    ([[], [], ['B12', 'z2'], ['B12', 'z2']], 'A6'),
    ([['B12'], ['B12'], ['v2', 'z3'], ['v2', 'z3']], 'A7'),
    ([['v3', 'B7', 'x1', 'B4', 'B6', 'B2'], ['v3', 'B7', 'x1', 'B4', 'B6', 'B2'], ['v3', 'x1', 'B4', 'B6', 'B2', 'B7'], ['v3', 'x1', 'B4', 'B6', 'B2', 'B7']], 'A13'),
    ([[], [], ['B13'], ['B13']], 'A16'),
    ([['B16'], ['B16'], [], []], 'A8'),
    ([['B8', 'B13'], ['B8', 'B13'], ['B16', 'B8'], ['B16', 'B8', 'C12']], 'A9'),
    ([[], [], [], []], 'A17'),
    ([['B17', 'x2', 'B1'], ['B17', 'x2', 'B1'], ['x2', 'B1'], ['B17', 'x2', 'B1']], 'A14'),
    ([[], [], ['B17', 'B14'], ['B14', 'D12']], 'A10'),
    ([['B10'], ['B10', 'B14'], ['B10'], ['B10']], 'A11'),
    ([['B14'], [], [], []], 'A18'),
    ([['B18', 'D12'], ['C12', 'B18', 'C7', 'D12', 'C16', 'x3', 'B3', 'B0', 'B5', 'B9', 'B11', 'D7'], ['B18', 'x3', 'B3', 'B0', 'B5', 'B9', 'B11', 'D12'], ['B18']], 'E12'),
    ([['D7', 'x3', 'B3', 'B0', 'B5', 'B9', 'B11'], [], [], ['x3', 'B3', 'B0', 'B5', 'B9', 'B11']], 'A15'),
    ([['D16', 'B15', 'D8', 'D4', 'D6'], ['C8', 'B15', 'D16', 'C4', 'D8', 'C6', 'D4', 'C2', 'D6'], ['B15'], ['B15']], 'A19'),
    ([[], [], ['B19', 'D4'], ['B19', 'C4', 'C6', 'D4', 'C2']], 'E4'),
    ([[], [], ['D6', 'D2', 'D7'], ['D6', 'C7', 'D2', 'C13', 'D7', 'C16']], 'E7'),
    ([[], ['C13'], [], []], 'E6'),
    ([[], [], ['D13', 'D16'], ['D13', 'C8', 'D16', 'C1']], 'E16'),
    ([['D2', 'B19'], ['B19', 'D2', 'C17'], [], []], 'E2'),
    ([[], [], ['D8'], ['D8', 'C17']], 'E8'),
    ([['D13'], ['D13', 'C10'], [], []], 'E13'),
    ([['D17'], ['D17', 'C1'], ['D1', 'D17'], ['D1', 'C14', 'D17', 'C10']], 'E17'),
    ([['D10', 'D1'], ['D10', 'C14', 'D1', 'C18'], [], []], 'E1'),
    ([[], [], ['D14', 'D10'], ['D14', 'C18', 'D10', 'C3']], 'E10'),
    ([['D14'], ['D14', 'C3'], [], []], 'E14'),
    ([['D18'], ['D18', 'C0'], ['D18'], ['D18', 'C0']], 'E18'),
    ([['D3'], ['D3', 'C5'], ['D3'], ['D3', 'C5']], 'E3'),
    ([['D0'], ['D0', 'C9'], ['D0'], ['D0', 'C9']], 'E0'),
    ([['D5'], ['D5', 'C11'], ['D5'], ['D5', 'C11']], 'E5'),
    ([['D9'], ['D9', 'C15'], ['D9'], ['D9', 'C15']], 'E9'),
    ([['D11'], ['D11', 'C19'], ['D11'], ['D11', 'C19']], 'E11'),
    ([['D15'], ['D15'], ['D15'], ['D15']], 'E15'),
    ([['D19'], ['D19'], ['D19'], ['D19']], 'E19'),
]


def split(value):
    high = value.astype(BF16)
    return high, (value - high.astype(F32)).astype(BF16)


def dot3(a_high, a_low, b_high, b_low):
    def one(a, b):
        return lax.dot_general(a, b, (((1,), (0,)), ((), ())), preferred_element_type=F32)

    return one(a_high, b_high) + (one(a_high, b_low) + one(a_low, b_high))


def kernel(sizes, own, grad, vis, own_th, own_tl, row_e, part, core_in, half, end_in, mid, mid_in, amp, via, *sems):
    rows, width, chunks, zl, n_x, n_q = sizes
    (ws, wr, x1s, x1r, x2s, x2r, zs, zr, x3s, x3r, c1s, c1r, es, er, ms, mr, ts, tr, c2s, c2r) = sems
    hw = width // 2
    aux, occ = lax.axis_index("aux"), lax.axis_index("occ")
    core, z_lo = lax.rem(aux, 2), aux // 2
    side, q = lax.rem(occ, 2), occ // 2

    def along(k):
        return (aux, lax.rem(q + k + n_q, n_q) * 2 + side)

    def at_z(z):
        return (z * 2 + core, occ)

    across = (aux, q * 2 + 1 - side)
    partner = (z_lo * 2 + 1 - core, occ)
    low_half = z_lo < zl // 2
    is_mid = (z_lo == zl // 2 - 1) | (z_lo == zl // 2)
    is_end = jnp.logical_not(is_mid)
    mid_of_end = jnp.where(low_half, 1, zl - 2)
    end_of_mid = jnp.where(low_half, 0, zl - 1)
    other_mid = jnp.where(low_half, zl - 2, 1)
    mine = pl.multiple_of(core * hw, hw)
    theirs = pl.multiple_of((1 - core) * hw, hw)

    def in_row(k, step):
        at = lax.rem(k + n_q, n_q)
        x_at = lax.rem(at, n_x)
        return (aux, (at - x_at + lax.rem(x_at + step, n_x)) * 2 + side)

    x2_from = in_row(q, 1)
    before = q - lax.rem(q, n_x) + lax.rem(lax.rem(q, n_x) + n_x - 1, n_x)
    w1_from = (aux, lax.rem(before - 2 + n_q, n_q) * 2 + side)

    barrier = pltpu.get_barrier_semaphore()

    def tell(device):
        pl.semaphore_signal(barrier, inc=1, device_id=device, device_id_type=MESH)

    for device in (along(-1), x2_from, w1_from, across, partner):
        tell(device)

    @pl.when(is_mid)
    def _():
        tell(at_z(end_of_mid))
        tell(at_z(other_mid))
        pl.semaphore_wait(barrier, 7)

    @pl.when(is_end)
    def _():
        tell(at_z(mid_of_end))
        pl.semaphore_wait(barrier, 6)

    def remote(src, dst, send, recv, device):
        return pltpu.make_async_remote_copy(src, dst, send, recv, device_id=device, device_id_type=MESH)

    def x1(c):
        return remote(own.at[c], vis.at[1, c], x1s.at[c], x1r.at[c], along(1))

    def w1(c):
        return remote(own.at[c], via.at[c], ws.at[c], wr.at[c], in_row(q + 2, 1))

    def x2(c):
        return remote(via.at[c], vis.at[3, c], x2s.at[c], x2r.at[c], in_row(q, n_x - 1))

    def z_own(c):
        return remote(own.at[c], vis.at[0, c], zs.at[c], zr.at[c], across)

    def z_vis(c):
        return remote(vis.at[1, c], vis.at[0, c], zs.at[c], zr.at[c], across)

    def x3(c):
        return remote(vis.at[0, c], vis.at[2, c], x3s.at[c], x3r.at[c], along(1))

    for c in range(chunks):
        x1(c).start()

        @pl.when(side == 0)
        def _():
            z_own(c).start()

    for c in range(chunks):
        w1(c).start()

    for c in range(chunks):
        high, low = split(own[c, :rows, :].T)
        own_th[pl.ds(c * LANES, LANES), :] = high
        own_tl[pl.ds(c * LANES, LANES), :] = low
        virt = own[c, pl.ds(rows + 1, 1), :]
        eps = own[c, pl.ds(rows, 1), :]
        row_e[pl.ds(c * LANES, LANES), :] = jnp.broadcast_to(virt - eps, (LANES, LANES)).T

    def visitor(d, c):
        return own.at[c] if d == 0 else vis.at[d - 1, c]

    def c1(u):
        d, c, n = UNITS[u]
        at = pl.ds(c, n)
        return remote(part.at[d, at, pl.ds(theirs, hw)], core_in.at[d, at], c1s.at[u], c1r.at[u], partner)

    def e(u):
        d, c, n = UNITS[u]
        at = pl.ds(c, n)
        return remote(half.at[d, at], end_in.at[d, at], es.at[u], er.at[u], at_z(mid_of_end))

    def m(u):
        d, c, n = UNITS[u]
        at = pl.ds(c, n)
        return remote(mid.at[d, at], mid_in.at[d, at], ms.at[u], mr.at[u], at_z(other_mid))

    def t(u):
        d, c, n = UNITS[u]
        block = amp.at[d, pl.ds(c, n), pl.ds(mine, hw)]
        return remote(block, block, ts.at[u], tr.at[u], at_z(end_of_mid))

    def c2(u):
        d, c, n = UNITS[u]
        block = amp.at[d, pl.ds(c, n), pl.ds(mine, hw)]
        return remote(block, block, c2s.at[u], c2r.at[u], partner)

    def joined(d, c, n):
        return jnp.concatenate([visitor(d, c + k)[:rows, :] for k in range(n)], axis=1)

    def stage_a(u):
        d, c, n = UNITS[u]
        for k in range(n):
            if d == 3:
                x3(c + k).wait_recv()
            if d == 4:
                x2(c + k).wait_recv()
            if d == 2:

                @pl.when(side == 0)
                def _():
                    x1(c + k).wait_recv()

        v_high, v_low = split(joined(d, c, n))

        @pl.loop(0, 2)
        def _(r):
            at = pl.ds(pl.multiple_of(r * hw, hw), hw)
            value = dot3(own_th[at, :], own_tl[at, :], v_high, v_low)
            for k in range(n):
                part[d, c + k, at, :] = value[:, k * LANES:(k + 1) * LANES]

        c1(u).start()

    def stage_b(u, middle):
        d, c, n = UNITS[u]
        c1(u).wait_recv()
        for k in range(n):
            half[d, c + k] = part[d, c + k, pl.ds(mine, hw), :] + core_in[d, c + k]
        if not middle:
            e(u).start()

    def stage_c(u, middle):
        d, c, n = UNITS[u]
        if middle:
            e(u).wait_recv()
            for k in range(n):
                mid[d, c + k] = half[d, c + k] + end_in[d, c + k]
            m(u).start()

    def stage_d(u, middle):
        d, c, n = UNITS[u]
        if middle:
            m(u).wait_recv()
            for k in range(n):
                total = mid[d, c + k] + mid_in[d, c + k]
                virt = own[c + k, pl.ds(rows + 1, 1), :]
                eps = visitor(d, c + k)[pl.ds(rows, 1), :]
                value = -total / (row_e[pl.ds(mine, hw), :] + (virt - eps))
                if d > 0:
                    live = own[c + k, pl.ds(rows + 1 + d, 1), :]
                    value = jnp.where(live > 0, value, jnp.zeros_like(value))
                amp[d, c + k, pl.ds(mine, hw), :] = value
            t(u).start()
        else:
            t(u).wait_recv()
        c2(u).start()

    def stage_e(u, first):
        d, c, n = UNITS[u]
        c2(u).wait_recv()
        t_high, t_low = split(jnp.concatenate([amp[d, c + k].T for k in range(n)], axis=0))
        step = rows // 4

        @pl.loop(0, 4)
        def _(r):
            at = pl.ds(pl.multiple_of(r * step, step), step)
            block = jnp.concatenate([visitor(d, c + k)[at, :] for k in range(n)], axis=1)
            v_high, v_low = split(block)
            value = dot3(v_high, v_low, t_high, t_low)
            if first:
                grad[at, :] = value
            else:
                grad[at, :] += value

    def stage_z(c):
        x1(c).wait_recv()
        z_vis(c).start()

    def stage_v(c):
        w1(c).wait_recv()
        x2(c).start()

    def stage_x(c):
        z_own(c).wait_recv()
        x3(c).start()

    def act(ops, middle):
        for op in ops:
            k = int(op[1:])
            if op[0] == "z":
                stage_z(k)
            elif op[0] == "v":
                stage_v(k)
            elif op[0] == "x":
                stage_x(k)
            else:
                {"B": stage_b, "C": stage_c, "D": stage_d}[op[0]](k, middle)

    kinds = [(side == 0) & is_end, (side == 0) & is_mid, (side == 1) & is_end, (side == 1) & is_mid]
    first = True
    for by_kind, common in PLAN:
        for kind, ops in enumerate(by_kind):
            if ops:
                pl.when(kinds[kind])(lambda ops=ops, kind=kind: act(ops, kind % 2 == 1))
        if common[:1] == "A":
            stage_a(int(common[1:]))
        if common[:1] == "E":
            stage_e(int(common[1:]), first)
            first = False

    for c in range(chunks):
        for copy in (x1, x2, z_own, x3, w1):
            copy(c).wait_send()
    for u in range(len(UNITS)):
        c1(u).wait_send()
        c2(u).wait_send()

        @pl.when(is_end)
        def _():
            e(u).wait_send()

        @pl.when(is_mid)
        def _():
            m(u).wait_send()
            t(u).wait_send()


def on_device(factors, eps_occ, eps_virt, pair_mask):
    rows, _, width = factors.shape
    chunks = width // LANES
    zl = lax.axis_size("aux") // 2
    n_q = lax.axis_size("occ") // 2
    group = lax.axis_index("occ")
    live = jnp.where(group >= jnp.arange(1, OFFSETS + 1), pair_mask[0], 0).astype(F32)
    blocks = factors.reshape(rows, chunks, LANES).transpose(1, 0, 2)
    extra = jnp.concatenate(
        [
            jnp.broadcast_to(eps_occ, (chunks, 1, LANES)),
            eps_virt.reshape(chunks, 1, LANES),
            jnp.broadcast_to(live[None, :, None], (chunks, OFFSETS, LANES)),
            jnp.zeros((chunks, PAD - 2 - OFFSETS, LANES), F32),
        ],
        axis=1,
    )
    own = jnp.concatenate([blocks, extra], axis=1)
    units, hw = len(UNITS), width // 2
    pairs = OFFSETS + 1
    dma = pltpu.SemaphoreType.DMA
    vmem = pltpu.VMEM
    sizes = (rows, width, chunks, zl, 4, n_q)
    grad = pl.pallas_call(
        lambda *refs: kernel(sizes, *refs),
        name="ri_mp2",
        out_shape=jax.ShapeDtypeStruct((rows, width), F32),
        in_specs=[pl.BlockSpec(memory_space=pltpu.VMEM)],
        out_specs=pl.BlockSpec(memory_space=pltpu.VMEM),
        scratch_shapes=[
            vmem((OFFSETS, chunks, rows + PAD, LANES), F32),
            vmem((width, rows), BF16),
            vmem((width, rows), BF16),
            vmem((width, LANES), F32),
            vmem((pairs, chunks, width, LANES), F32),
            vmem((pairs, chunks, hw, LANES), F32),
            vmem((pairs, chunks, hw, LANES), F32),
            vmem((pairs, chunks, hw, LANES), F32),
            vmem((pairs, chunks, hw, LANES), F32),
            vmem((pairs, chunks, hw, LANES), F32),
            vmem((pairs, chunks, width, LANES), F32),
            vmem((chunks, rows + PAD, LANES), F32),
        ]
        + [dma((chunks,))] * 10
        + [dma((units,))] * 10,
        compiler_params=pltpu.CompilerParams(
            collective_id=0, has_side_effects=True, vmem_limit_bytes=60 * 1024 * 1024
        ),
    )(own)
    return grad.reshape(factors.shape)


def solution(mesh):
    in_specs = (P("aux", "occ", None), P("occ"), P(), P("occ", None))
    out_specs = P("aux", "occ", None)
    return jax.shard_map(
        on_device, mesh=mesh, in_specs=in_specs, out_specs=out_specs, check_vma=False
    )
```

```python
import jax
import jax.numpy as jnp
from jax import lax
from jax.experimental import pallas as pl
from jax.experimental.pallas import tpu as pltpu
from jax.sharding import PartitionSpec as P

OFFSETS = 4
LANES = 128
PAD = 8
MESH = pl.DeviceIdType.MESH
F32 = jnp.float32
BF16 = jnp.bfloat16

UNITS = [(0, 0, 1), (0, 1, 1), (0, 2, 1), (0, 3, 1), (2, 0, 2), (2, 2, 2), (4, 0, 1), (4, 1, 1), (4, 2, 1), (4, 3, 1), (1, 0, 2), (1, 2, 2), (3, 0, 1), (3, 1, 1), (3, 2, 1), (3, 3, 1)]
EARLY = 4
PLAN = [
    ([[], [], [], []], 'A1'),
    ([[], [], [], []], 'A0'),
    ([[], [], [], []], 'A2'),
    ([[], [], ['B1'], ['B1']], 'A3'),
    ([['v0'], ['v0'], ['z0', 'v0', 'z1'], ['C1', 'z0', 'v0', 'D1', 'z1']], 'A4'),
    ([['v1', 'v2', 'x0', 'B1'], ['v1', 'v2', 'x0', 'B1'], ['v1', 'x0', 'z2', 'v2', 'D1', 'z3'], ['v1', 'x0', 'z2', 'v2', 'z3']], 'A5'),
    ([['v3', 'B5', 'x1'], ['v3', 'B5', 'x1'], ['v3', 'x1'], ['v3', 'x1']], 'A10'),
    ([[], [], ['B5', 'B10'], ['B5', 'B10']], 'A12'),
    ([['B12'], ['B12'], [], []], 'A6'),
    ([['B6', 'B10'], ['B6', 'B10'], ['B12', 'B6'], ['B12', 'B6']], 'A7'),
    ([[], [], [], []], 'A13'),
    ([['B13'], ['B13'], ['x2', 'B4', 'B13'], ['x2', 'B4', 'B13']], 'A8'),
    ([['B8', 'x2', 'B3', 'B4'], ['B8', 'x2', 'B3', 'B4', 'C1', 'D1'], ['B8'], ['B8']], 'A14'),
    ([[], [], ['B14'], ['B14']], 'A9'),
    ([['B14', 'D1', 'x3', 'B0', 'B7', 'B9', 'B2'], ['B14', 'C5', 'C12', 'x3', 'B0', 'B7', 'B9', 'B2'], ['x3', 'B0', 'B7', 'B2', 'B3'], ['x3', 'B0', 'B7', 'B2', 'B3']], 'A11'),
    ([['B11'], ['C6', 'D5', 'B11', 'D12', 'C10', 'D6', 'C13'], ['B9', 'B11'], ['B9', 'B11']], 'A15'),
    ([['D5', 'B15'], [], ['B15', 'D5'], ['B15', 'C5', 'C10', 'D5', 'C12']], 'E5'),
    ([['D12', 'D6'], [], ['D10', 'D12'], ['C6', 'D10', 'D12', 'C4', 'D6']], 'E12'),
    ([[], [], ['D6'], ['C13']], 'E6'),
    ([['D10'], ['C8', 'B15', 'D10', 'C3'], [], []], 'E10'),
    ([['D13'], ['D13', 'D8'], ['D4', 'D13'], ['C8', 'D4', 'C14', 'C0', 'D13', 'C7', 'D8']], 'E13'),
    ([['D8'], ['C4'], ['D8'], ['C2']], 'E8'),
    ([['D3', 'D4', 'D0'], ['D3', 'C14', 'C0', 'C7', 'D4', 'C9'], [], []], 'E4'),
    ([['D14'], ['D0', 'D14', 'C2'], ['D0', 'D14'], ['D14', 'C3', 'D0']], 'E14'),
    ([['D7'], ['D7', 'C11', 'D9'], ['D7'], ['C9', 'D7']], 'E7'),
    ([['D9', 'D2'], ['D2', 'C15'], ['D2', 'D3'], ['D2', 'D3', 'C11']], 'E3'),
    ([[], [], ['D9'], ['D9', 'C15']], 'E9'),
    ([['D11'], ['D11'], ['D11'], ['D11']], 'E11'),
    ([['D15'], ['D15'], ['D15'], ['D15']], 'E15'),
]


def split(value):
    high = value.astype(BF16)
    return high, (value - high.astype(F32)).astype(BF16)


def dot3(a_high, a_low, b_high, b_low):
    def one(a, b):
        return lax.dot_general(a, b, (((1,), (0,)), ((), ())), preferred_element_type=F32)

    return one(a_high, b_high) + (one(a_high, b_low) + one(a_low, b_high))


def kernel(sizes, factors, eps_virt, eps_occ, mask, out, own, grad, vis, own_th, own_tl, row_e, part, core_in, half, end_in, mid, mid_in, amp, via, *sems):
    rows, width, chunks, zl, n_x, n_q = sizes
    (ws, wr, x1s, x1r, x2s, x2r, zs, zr, x3s, x3r, c1s, c1r, es, er, ms, mr, ts, tr, c2s, c2r) = sems
    hw = width // 2
    aux, occ = lax.axis_index("aux"), lax.axis_index("occ")
    core, z_lo = lax.rem(aux, 2), aux // 2
    side, q = lax.rem(occ, 2), occ // 2

    def along(k):
        return (aux, lax.rem(q + k + n_q, n_q) * 2 + side)

    def at_z(z):
        return (z * 2 + core, occ)

    across = (aux, q * 2 + 1 - side)
    partner = (z_lo * 2 + 1 - core, occ)
    low_half = z_lo < zl // 2
    is_mid = (z_lo == zl // 2 - 1) | (z_lo == zl // 2)
    is_end = jnp.logical_not(is_mid)
    mid_of_end = jnp.where(low_half, 1, zl - 2)
    end_of_mid = jnp.where(low_half, 0, zl - 1)
    other_mid = jnp.where(low_half, zl - 2, 1)

    def rows_of(u):
        d, c, n = UNITS[u]
        return (c + 1) * LANES if d == 0 else width

    def share(u, which):
        size = rows_of(u) // 2
        return pl.ds(pl.multiple_of(which * size, size), size)

    def mine(u):
        return share(u, core)

    def theirs(u):
        return share(u, 1 - core)

    def first_rows(u):
        return pl.ds(0, rows_of(u) // 2)

    def in_row(k, step):
        at = lax.rem(k + n_q, n_q)
        x_at = lax.rem(at, n_x)
        return (aux, (at - x_at + lax.rem(x_at + step, n_x)) * 2 + side)

    x2_from = in_row(q, 1)
    before = q - lax.rem(q, n_x) + lax.rem(lax.rem(q, n_x) + n_x - 1, n_x)
    w1_from = (aux, lax.rem(before - 2 + n_q, n_q) * 2 + side)

    barrier = pltpu.get_barrier_semaphore()

    def tell(device):
        pl.semaphore_signal(barrier, inc=1, device_id=device, device_id_type=MESH)

    for device in (along(-1), x2_from, w1_from, across, partner):
        tell(device)

    @pl.when(is_mid)
    def _():
        tell(at_z(end_of_mid))
        tell(at_z(other_mid))

    @pl.when(is_end)
    def _():
        tell(at_z(mid_of_end))

    eps = jnp.full((1, LANES), eps_occ[0], F32)
    live = [
        jnp.full((1, LANES), jnp.where(occ >= d, mask[0, d - 1], 0), jnp.int32).astype(F32)
        for d in range(1, OFFSETS + 1)
    ]
    blank = jnp.zeros((PAD - 2 - OFFSETS, LANES), F32)
    for c in range(chunks):
        own[c, pl.ds(0, rows), :] = factors[pl.ds(c, rows, stride=chunks), :]
        own[c, pl.ds(rows, PAD), :] = jnp.concatenate([eps, eps_virt[pl.ds(c, 1), :], *live, blank], axis=0)

    @pl.when(is_mid)
    def _():
        pl.semaphore_wait(barrier, 7)

    @pl.when(is_end)
    def _():
        pl.semaphore_wait(barrier, 6)

    def remote(src, dst, send, recv, device):
        return pltpu.make_async_remote_copy(src, dst, send, recv, device_id=device, device_id_type=MESH)

    def x1(c):
        return remote(own.at[c], vis.at[1, c], x1s.at[c], x1r.at[c], along(1))

    def w1(c):
        return remote(own.at[c], via.at[c], ws.at[c], wr.at[c], in_row(q + 2, 1))

    def x2(c):
        return remote(via.at[c], vis.at[3, c], x2s.at[c], x2r.at[c], in_row(q, n_x - 1))

    def z_own(c):
        return remote(own.at[c], vis.at[0, c], zs.at[c], zr.at[c], across)

    def z_vis(c):
        return remote(vis.at[1, c], vis.at[0, c], zs.at[c], zr.at[c], across)

    def x3(c):
        return remote(vis.at[0, c], vis.at[2, c], x3s.at[c], x3r.at[c], along(1))

    for c in range(chunks):
        x1(c).start()
        if c < EARLY:

            @pl.when(side == 0)
            def _():
                z_own(c).start()

    for c in range(chunks):
        w1(c).start()

    for c in range(chunks):
        high, low = split(own[c, :rows, :].T)
        own_th[pl.ds(c * LANES, LANES), :] = high
        own_tl[pl.ds(c * LANES, LANES), :] = low
        virt = own[c, pl.ds(rows + 1, 1), :]
        eps = own[c, pl.ds(rows, 1), :]
        row_e[pl.ds(c * LANES, LANES), :] = jnp.broadcast_to(virt - eps, (LANES, LANES)).T

    def visitor(d, c):
        return own.at[c] if d == 0 else vis.at[d - 1, c]

    def c1(u):
        d, c, n = UNITS[u]
        at = pl.ds(c, n)
        return remote(part.at[d, at, theirs(u)], core_in.at[d, at, first_rows(u)], c1s.at[u], c1r.at[u], partner)

    def e(u):
        d, c, n = UNITS[u]
        at = pl.ds(c, n)
        return remote(half.at[d, at, first_rows(u)], end_in.at[d, at, first_rows(u)], es.at[u], er.at[u], at_z(mid_of_end))

    def m(u):
        d, c, n = UNITS[u]
        at = pl.ds(c, n)
        return remote(mid.at[d, at, first_rows(u)], mid_in.at[d, at, first_rows(u)], ms.at[u], mr.at[u], at_z(other_mid))

    def t(u):
        d, c, n = UNITS[u]
        block = amp.at[d, pl.ds(c, n), mine(u)]
        return remote(block, block, ts.at[u], tr.at[u], at_z(end_of_mid))

    def c2(u):
        d, c, n = UNITS[u]
        block = amp.at[d, pl.ds(c, n), mine(u)]
        return remote(block, block, c2s.at[u], c2r.at[u], partner)

    def joined(d, c, n):
        return jnp.concatenate([visitor(d, c + k)[:rows, :] for k in range(n)], axis=1)

    def stage_a(u):
        d, c, n = UNITS[u]
        for k in range(n):
            if d == 3:
                x3(c + k).wait_recv()
            if d == 4:
                x2(c + k).wait_recv()
            if d == 2:

                @pl.when(side == 0)
                def _():
                    x1(c + k).wait_recv()

        v_high, v_low = split(joined(d, c, n))

        at = pl.ds(0, rows_of(u))
        value = dot3(own_th[at, :], own_tl[at, :], v_high, v_low)
        for k in range(n):
            part[d, c + k, at, :] = value[:, k * LANES:(k + 1) * LANES]
        c1(u).start()

    def stage_b(u, middle):
        d, c, n = UNITS[u]
        c1(u).wait_recv()
        for k in range(n):
            half[d, c + k, first_rows(u), :] = part[d, c + k, mine(u), :] + core_in[d, c + k, first_rows(u), :]
        if not middle:
            e(u).start()

    def stage_c(u, middle):
        d, c, n = UNITS[u]
        if middle:
            e(u).wait_recv()
            for k in range(n):
                mid[d, c + k, first_rows(u), :] = half[d, c + k, first_rows(u), :] + end_in[d, c + k, first_rows(u), :]
            m(u).start()

    def stage_d(u, middle):
        d, c, n = UNITS[u]
        if middle:
            m(u).wait_recv()
            for k in range(n):
                total = mid[d, c + k, first_rows(u), :] + mid_in[d, c + k, first_rows(u), :]
                virt = own[c + k, pl.ds(rows + 1, 1), :]
                eps = visitor(d, c + k)[pl.ds(rows, 1), :]
                value = -total / (row_e[mine(u), :] + (virt - eps))
                if d > 0:
                    live = own[c + k, pl.ds(rows + 1 + d, 1), :]
                    value = jnp.where(live > 0, value, jnp.zeros_like(value))
                amp[d, c + k, mine(u), :] = value
            t(u).start()
        else:
            t(u).wait_recv()
        c2(u).start()

    def transposed(d, c):
        if d > 0:
            return amp[d, c].T
        blocks = [
            amp[0, c, pl.ds(r * LANES, LANES), :].T if r <= c else amp[0, r, pl.ds(c * LANES, LANES), :]
            for r in range(chunks)
        ]
        return jnp.concatenate(blocks, axis=1)

    def stage_e(u, first, last):
        d, c, n = UNITS[u]
        if d == 0:
            for k in range(u + 1):
                c2(k).wait_recv()
            c, n = 0, chunks
        else:
            c2(u).wait_recv()
        t_high, t_low = split(jnp.concatenate([transposed(d, c + k) for k in range(n)], axis=0))
        steps = 2
        step = rows // steps

        def contracted(at):
            block = jnp.concatenate([visitor(d, c + k)[at, :] for k in range(n)], axis=1)
            v_high, v_low = split(block)
            value = dot3(v_high, v_low, t_high, t_low)
            return value if first else grad[at, :] + value

        if last:
            for r in range(steps):
                value = contracted(pl.ds(r * step, step))
                for k in range(chunks):
                    out[pl.ds(r * step * chunks + k, step, stride=chunks), :] = value[:, k * LANES:(k + 1) * LANES]
        else:

            @pl.loop(0, steps)
            def _(r):
                at = pl.ds(pl.multiple_of(r * step, step), step)
                grad[at, :] = contracted(at)

    def stage_z(c):
        x1(c).wait_recv()
        z_vis(c).start()

    def stage_v(c):
        w1(c).wait_recv()
        x2(c).start()

    def stage_x(c):
        z_own(c).wait_recv()
        x3(c).start()

    def act(ops, middle):
        for op in ops:
            k = int(op[1:])
            if op[0] == "y":
                z_own(k).start()
            elif op[0] == "z":
                stage_z(k)
            elif op[0] == "v":
                stage_v(k)
            elif op[0] == "x":
                stage_x(k)
            else:
                {"B": stage_b, "C": stage_c, "D": stage_d}[op[0]](k, middle)

    kinds = [(side == 0) & is_end, (side == 0) & is_mid, (side == 1) & is_end, (side == 1) & is_mid]
    order = [common for _, common in PLAN if common[:1] == "E"]
    for by_kind, common in PLAN:
        for kind, ops in enumerate(by_kind):
            if ops:
                pl.when(kinds[kind])(lambda ops=ops, kind=kind: act(ops, kind % 2 == 1))
        if common[:1] == "A":
            stage_a(int(common[1:]))
        if common[:1] == "E":
            stage_e(int(common[1:]), common == order[0], common == order[-1])

    for c in range(chunks):
        for copy in (x1, x2, z_own, x3, w1):
            copy(c).wait_send()
    for u in range(len(UNITS)):
        c1(u).wait_send()
        c2(u).wait_send()

        @pl.when(is_end)
        def _():
            e(u).wait_send()

        @pl.when(is_mid)
        def _():
            m(u).wait_send()
            t(u).wait_send()


def write_out(source, result, done):
    step = source.shape[0] // done.shape[0]
    copies = []
    for k in range(done.shape[0]):
        at = pl.ds(k * step, step)
        copies.append(pltpu.make_async_copy(source.at[at], result.at[at], done.at[k]))
    for copy in copies:
        copy.start()
    for copy in copies:
        copy.wait()


def on_device(factors, eps_occ, eps_virt, pair_mask):
    rows, _, width = factors.shape
    chunks = width // LANES
    zl = lax.axis_size("aux") // 2
    n_q = lax.axis_size("occ") // 2
    units, hw = len(UNITS), width // 2
    pairs = OFFSETS + 1
    dma = pltpu.SemaphoreType.DMA
    vmem = pltpu.VMEM
    sizes = (rows, width, chunks, zl, 4, n_q)
    in_vmem = pl.BlockSpec(memory_space=pltpu.VMEM)
    in_smem = pl.BlockSpec(memory_space=pltpu.SMEM)
    grad = pl.pallas_call(
        lambda *refs: kernel(sizes, *refs),
        name="ri_mp2",
        out_shape=jax.ShapeDtypeStruct((rows * chunks, LANES), F32),
        in_specs=[in_vmem, in_vmem, in_smem, in_smem],
        out_specs=in_vmem,
        scratch_shapes=[
            vmem((chunks, rows + PAD, LANES), F32),
            vmem((rows, width), F32),
            vmem((OFFSETS, chunks, rows + PAD, LANES), F32),
            vmem((width, rows), BF16),
            vmem((width, rows), BF16),
            vmem((width, LANES), F32),
            vmem((pairs, chunks, width, LANES), F32),
            vmem((pairs, chunks, hw, LANES), F32),
            vmem((pairs, chunks, hw, LANES), F32),
            vmem((pairs, chunks, hw, LANES), F32),
            vmem((pairs, chunks, hw, LANES), F32),
            vmem((pairs, chunks, hw, LANES), F32),
            vmem((pairs, chunks, width, LANES), F32),
            vmem((chunks, rows + PAD, LANES), F32),
        ]
        + [dma((chunks,))] * 10
        + [dma((units,))] * 10,
        compiler_params=pltpu.CompilerParams(
            collective_id=0, has_side_effects=True, vmem_limit_bytes=60 * 1024 * 1024
        ),
    )(factors.reshape(rows * chunks, LANES), eps_virt.reshape(chunks, LANES), eps_occ, pair_mask)
    result = pl.pallas_call(
        write_out,
        name="write_out",
        out_shape=jax.ShapeDtypeStruct(grad.shape, F32),
        in_specs=[in_vmem],
        out_specs=pl.BlockSpec(memory_space=pl.ANY),
        scratch_shapes=[dma((8,))],
    )(grad)
    return result.reshape(factors.shape)


def solution(mesh):
    in_specs = (P("aux", "occ", None), P("occ"), P(), P("occ", None))
    out_specs = P("aux", "occ", None)
    return jax.shard_map(
        on_device, mesh=mesh, in_specs=in_specs, out_specs=out_specs, check_vma=False
    )
```

```python
import jax
import jax.numpy as jnp
from jax import lax
from jax.experimental import pallas as pl
from jax.experimental.pallas import tpu as pltpu
from jax.sharding import PartitionSpec as P

OFFSETS = 4
LANES = 128
PAD = 8
VMEM_MIB = 48
MESH = pl.DeviceIdType.MESH
F32 = jnp.float32
BF16 = jnp.bfloat16

UNITS = [(0, 0, 1, 0, 128), (0, 1, 1, 0, 256), (0, 2, 1, 0, 384), (0, 3, 1, 0, 512), (2, 0, 1, 0, 512), (2, 1, 1, 0, 512), (2, 2, 1, 0, 256), (2, 2, 1, 256, 512), (2, 3, 1, 0, 256), (2, 3, 1, 256, 512), (4, 0, 1, 0, 512), (4, 1, 1, 0, 512), (4, 2, 1, 0, 256), (4, 2, 1, 256, 512), (4, 3, 1, 0, 256), (4, 3, 1, 256, 512), (1, 0, 2, 0, 512), (1, 2, 1, 0, 512), (1, 3, 1, 0, 512), (3, 0, 1, 0, 512), (3, 1, 1, 0, 512), (3, 2, 1, 0, 512), (3, 3, 1, 0, 256), (3, 3, 1, 256, 512)]
EARLY = 6
PLAN = [
    ([[], [], [], []], 'A2'),
    ([[], [], [], []], 'A1'),
    ([[], [], [], []], 'A3'),
    ([[], [], [], []], 'A0'),
    ([['B0'], ['B0'], ['z0', 'z1', 'z2'], ['z0', 'z1', 'z2']], 'A4'),
    ([['v0'], ['v0'], ['v0', 'z3'], ['v0', 'z3']], 'A5'),
    ([['v1', 'x0'], ['v1', 'x0'], ['v1', 'x0', 'z4'], ['v1', 'x0', 'z4']], 'A6'),
    ([['v2'], ['v2'], ['v2'], ['v2']], 'A7'),
    ([[], [], ['z5'], ['z5']], 'A8'),
    ([['v3'], ['v3'], ['v3'], ['v3']], 'A9'),
    ([['x1', 'B2'], ['x1', 'B2'], ['x1', 'B2'], ['x1', 'B2']], 'A16'),
    ([['B16'], ['B16'], ['B16'], ['B16']], 'A19'),
    ([[], [], [], []], 'A10'),
    ([['B19'], ['B19'], ['B19'], ['B19']], 'A20'),
    ([[], [], [], []], 'A11'),
    ([['B20', 'B11', 'x2', 'B1', 'B3'], ['B20', 'B11', 'x2', 'B1', 'B3'], ['x2', 'B1', 'B3', 'B0', 'B20'], ['x2', 'B1', 'B3', 'B0', 'B20']], 'A17'),
    ([['B17'], ['B17'], ['B11', 'B17'], ['B11', 'B17']], 'A12'),
    ([[], [], [], []], 'A13'),
    ([['B12', 'B13'], ['B12', 'B13'], ['B12', 'B13'], ['B12', 'B13']], 'A21'),
    ([['B21'], ['B21'], ['B21'], ['B21']], 'A14'),
    ([[], [], [], []], 'A15'),
    ([['x3', 'B10', 'B6', 'B7', 'D0', 'B5', 'B8', 'B9', 'B4', 'B14', 'B15'], ['C0', 'D0', 'C2', 'x3', 'B10', 'B6', 'B7', 'B5', 'B8', 'B9', 'B4', 'B14', 'B15'], ['B14', 'x3', 'B10', 'B6', 'B7', 'B5', 'B8', 'B9', 'B4', 'B15'], ['B14', 'x3', 'B10', 'B6', 'B7', 'B5', 'B8', 'B9', 'B4', 'B15']], 'A18'),
    ([['B18', 'D2'], ['D2', 'B18', 'C16', 'C19', 'C20', 'D16', 'C11'], ['B18', 'D2'], ['B18', 'C2', 'D2', 'C16']], 'A22'),
    ([[], [], [], ['C19']], 'A23'),
    ([['B22', 'B23', 'D16'], ['C1'], ['B22', 'B23', 'D16'], ['C1', 'B22', 'B23', 'C3', 'D16', 'C0']], 'E16'),
    ([['D19'], ['D19', 'B22', 'B23', 'C3', 'D20'], ['D19', 'D1'], ['D19', 'D1', 'C20']], 'E19'),
    ([['D20'], [], ['D3', 'D0', 'D20'], ['D3', 'C11', 'D0', 'C17', 'D20', 'C12', 'C13']], 'E20'),
    ([['D11', 'D1', 'D3'], ['D11', 'C17', 'C12', 'D1', 'C13', 'D3', 'C21'], [], []], 'E3'),
    ([[], [], ['D11'], ['D11', 'C21', 'C14', 'D17']], 'E11'),
    ([['D17', 'D12'], ['D17', 'D12', 'C10', 'C6', 'D13'], ['D17', 'D12'], ['D12']], 'E17'),
    ([['D13'], ['C7'], ['D13'], ['D13', 'C10', 'C6']], 'E13'),
    ([['D21'], ['D21', 'C5'], ['D21', 'D14'], ['D21', 'C7', 'D14']], 'E21'),
    ([['D10', 'D6'], ['D10', 'C8', 'C9', 'D6'], ['D10', 'D6'], ['C5', 'C8', 'D10', 'C9', 'D6']], 'E10'),
    ([['D7'], ['D7', 'C4'], ['D7'], ['D7', 'C4']], 'E7'),
    ([['D5', 'D8'], ['D5', 'C14', 'C15', 'D8'], ['D5', 'D8'], ['D5', 'C15', 'D8']], 'E5'),
    ([['D9'], ['D9', 'C18'], ['D9'], ['D9', 'C18', 'C22']], 'E9'),
    ([['D4', 'D14'], ['D4', 'C22', 'C23', 'D14'], ['D4', 'D15'], ['D4', 'C23', 'D15']], 'E4'),
    ([['D15'], ['D15'], [], []], 'E15'),
    ([['D18', 'D22'], ['D18', 'D22'], ['D18', 'D22'], ['D18', 'D22']], 'E18'),
    ([['D23'], ['D23'], ['D23'], ['D23']], 'E23'),
]

PIECES = [(0, 0, 256), (0, 256, 256), (0, 512, 512 + PAD), (1, 0, 1024), (2, 0, 1024), (3, 0, 1024)]


def split(value):
    high = value.astype(BF16)
    return high, (value - high.astype(F32)).astype(BF16)


def dot3(a_high, a_low, b_high, b_low):
    def one(a, b):
        return lax.dot_general(a, b, (((1,), (0,)), ((), ())), preferred_element_type=F32)

    return one(a_high, b_high) + (one(a_high, b_low) + one(a_low, b_high))


def kernel(sizes, factors, eps_virt, eps_occ, mask, out, own, grad, vis, own_th, own_tl, row_e, part, core_in, half, end_in, mid, mid_in, amp, via, *sems):
    rows, width, chunks, zl, n_x, n_q = sizes
    (ws, wr, x1s, x1r, x2s, x2r, zs, zr, x3s, x3r, c1s, c1r, es, er, ms, mr, ts, tr, c2s, c2r) = sems
    hw = width // 2
    aux, occ = lax.axis_index("aux"), lax.axis_index("occ")
    core, z_lo = lax.rem(aux, 2), aux // 2
    side, q = lax.rem(occ, 2), occ // 2

    def along(k):
        return (aux, lax.rem(q + k + n_q, n_q) * 2 + side)

    def at_z(z):
        return (z * 2 + core, occ)

    across = (aux, q * 2 + 1 - side)
    partner = (z_lo * 2 + 1 - core, occ)
    low_half = z_lo < zl // 2
    is_mid = (z_lo == zl // 2 - 1) | (z_lo == zl // 2)
    is_end = jnp.logical_not(is_mid)
    mid_of_end = jnp.where(low_half, 1, zl - 2)
    end_of_mid = jnp.where(low_half, 0, zl - 1)
    other_mid = jnp.where(low_half, zl - 2, 1)

    def rows_of(u):
        return UNITS[u][4] - UNITS[u][3]

    def share(u, which):
        size = rows_of(u) // 2
        return pl.ds(pl.multiple_of(UNITS[u][3] + which * size, size), size)

    def mine(u):
        return share(u, core)

    def theirs(u):
        return share(u, 1 - core)

    def first_rows(u):
        return pl.ds(UNITS[u][3] // 2, rows_of(u) // 2)

    def in_row(k, step):
        at = lax.rem(k + n_q, n_q)
        x_at = lax.rem(at, n_x)
        return (aux, (at - x_at + lax.rem(x_at + step, n_x)) * 2 + side)

    x2_from = in_row(q, 1)
    before = q - lax.rem(q, n_x) + lax.rem(lax.rem(q, n_x) + n_x - 1, n_x)
    w1_from = (aux, lax.rem(before - 2 + n_q, n_q) * 2 + side)

    barrier = pltpu.get_barrier_semaphore()

    def tell(device):
        pl.semaphore_signal(barrier, inc=1, device_id=device, device_id_type=MESH)

    for device in (along(-1), x2_from, w1_from, across, partner):
        tell(device)

    @pl.when(is_mid)
    def _():
        tell(at_z(end_of_mid))
        tell(at_z(other_mid))

    @pl.when(is_end)
    def _():
        tell(at_z(mid_of_end))

    eps = jnp.full((1, LANES), eps_occ[0], F32)
    live = [
        jnp.full((1, LANES), jnp.where(occ >= d, mask[0, d - 1], 0), jnp.int32).astype(F32)
        for d in range(1, OFFSETS + 1)
    ]
    blank = jnp.zeros((PAD - 2 - OFFSETS, LANES), F32)
    for c in range(chunks):
        own[c, pl.ds(0, rows), :] = factors[pl.ds(c, rows, stride=chunks), :]
        own[c, pl.ds(rows, PAD), :] = jnp.concatenate([eps, eps_virt[pl.ds(c, 1), :], *live, blank], axis=0)

    @pl.when(is_mid)
    def _():
        pl.semaphore_wait(barrier, 7)

    @pl.when(is_end)
    def _():
        pl.semaphore_wait(barrier, 6)

    def remote(src, dst, send, recv, device):
        return pltpu.make_async_remote_copy(src, dst, send, recv, device_id=device, device_id_type=MESH)

    def full(c):
        return pl.ds(0, rows + PAD if c == 0 else rows)

    def piece(ref, p, *slot):
        c, row, size = PIECES[p]
        return ref.at[(*slot, c, pl.ds(row, size))]

    def pieces_of(c):
        return [p for p, item in enumerate(PIECES) if item[0] == c]

    def x1(p):
        return remote(piece(own, p), piece(vis, p, 1), x1s.at[p], x1r.at[p], along(1))

    def w1(c):
        return remote(own.at[c, full(c)], via.at[c, full(c)], ws.at[c], wr.at[c], in_row(q + 2, 1))

    def x2(c):
        return remote(via.at[c, full(c)], vis.at[3, c, full(c)], x2s.at[c], x2r.at[c], in_row(q, n_x - 1))

    def z_own(p):
        return remote(piece(own, p), piece(vis, p, 0), zs.at[p], zr.at[p], across)

    def z_vis(p):
        return remote(piece(vis, p, 1), piece(vis, p, 0), zs.at[p], zr.at[p], across)

    def x3(c):
        return remote(vis.at[0, c, full(c)], vis.at[2, c, full(c)], x3s.at[c], x3r.at[c], along(1))

    def first_hop(p):
        x1(p).start()
        if p < EARLY:

            @pl.when(side == 0)
            def _():
                z_own(p).start()

    for p in range(len(PIECES)):
        if p == 4:
            w1(0).start()
        first_hop(p)
    for c in range(1, chunks):
        w1(c).start()

    for c in range(chunks):
        high, low = split(own[c, :rows, :].T)
        own_th[pl.ds(c * LANES, LANES), :] = high
        own_tl[pl.ds(c * LANES, LANES), :] = low
        virt = own[c, pl.ds(rows + 1, 1), :]
        eps = own[c, pl.ds(rows, 1), :]
        row_e[pl.ds(c * LANES, LANES), :] = jnp.broadcast_to(virt - eps, (LANES, LANES)).T

    def visitor(d, c):
        return own.at[c] if d == 0 else vis.at[d - 1, c]

    def c1(u):
        d, c, n = UNITS[u][:3]
        at = pl.ds(c, n)
        return remote(part.at[d, at, theirs(u)], core_in.at[d, at, first_rows(u)], c1s.at[u], c1r.at[u], partner)

    def e(u):
        d, c, n = UNITS[u][:3]
        at = pl.ds(c, n)
        return remote(half.at[d, at, first_rows(u)], end_in.at[d, at, first_rows(u)], es.at[u], er.at[u], at_z(mid_of_end))

    def m(u):
        d, c, n = UNITS[u][:3]
        at = pl.ds(c, n)
        return remote(mid.at[d, at, first_rows(u)], mid_in.at[d, at, first_rows(u)], ms.at[u], mr.at[u], at_z(other_mid))

    def t(u):
        d, c, n = UNITS[u][:3]
        block = amp.at[d, pl.ds(c, n), mine(u)]
        return remote(block, block, ts.at[u], tr.at[u], at_z(end_of_mid))

    def c2(u):
        d, c, n = UNITS[u][:3]
        block = amp.at[d, pl.ds(c, n), mine(u)]
        return remote(block, block, c2s.at[u], c2r.at[u], partner)

    def joined(d, c, n):
        return jnp.concatenate([visitor(d, c + k)[:rows, :] for k in range(n)], axis=1)

    arrived = set()

    def stage_a(u):
        d, c, n = UNITS[u][:3]
        for k in range(c, c + n):
            if (d, k) in arrived:
                continue
            arrived.add((d, k))
            if d == 3:
                x3(k).wait_recv()
            if d == 4:
                x2(k).wait_recv()
            if d == 2:

                @pl.when(side == 0)
                def _():
                    for p in pieces_of(k):
                        x1(p).wait_recv()

        v_high, v_low = split(joined(d, c, n))

        at = pl.ds(UNITS[u][3], rows_of(u))
        value = dot3(own_th[at, :], own_tl[at, :], v_high, v_low)
        for k in range(n):
            part[d, c + k, at, :] = value[:, k * LANES:(k + 1) * LANES]
        c1(u).start()

    def stage_b(u, middle):
        d, c, n = UNITS[u][:3]
        c1(u).wait_recv()
        for k in range(n):
            half[d, c + k, first_rows(u), :] = part[d, c + k, mine(u), :] + core_in[d, c + k, first_rows(u), :]
        if not middle:
            e(u).start()

    def stage_c(u, middle):
        d, c, n = UNITS[u][:3]
        if middle:
            e(u).wait_recv()
            for k in range(n):
                mid[d, c + k, first_rows(u), :] = half[d, c + k, first_rows(u), :] + end_in[d, c + k, first_rows(u), :]
            m(u).start()

    def stage_d(u, middle):
        d, c, n = UNITS[u][:3]
        if middle:
            m(u).wait_recv()
            for k in range(n):
                total = mid[d, c + k, first_rows(u), :] + mid_in[d, c + k, first_rows(u), :]
                virt = own[c + k, pl.ds(rows + 1, 1), :]
                eps = visitor(d, 0)[pl.ds(rows, 1), :]
                value = -total / (row_e[mine(u), :] + (virt - eps))
                if d > 0:
                    live = own[c + k, pl.ds(rows + 1 + d, 1), :]
                    value = jnp.where(live > 0, value, jnp.zeros_like(value))
                amp[d, c + k, mine(u), :] = value
            t(u).start()
        else:
            t(u).wait_recv()
        c2(u).start()

    def transposed(d, c):
        if d > 0:
            return amp[d, c].T
        blocks = [
            amp[0, c, pl.ds(r * LANES, LANES), :].T if r <= c else amp[0, r, pl.ds(c * LANES, LANES), :]
            for r in range(chunks)
        ]
        return jnp.concatenate(blocks, axis=1)

    def stage_e(u, first, last):
        d, c, n = UNITS[u][:3]
        for k, other in enumerate(UNITS):
            if other[0] == d and (d == 0 or other[1] == c):
                c2(k).wait_recv()
        if d == 0:
            c, n = 0, chunks
        t_high, t_low = split(jnp.concatenate([transposed(d, c + k) for k in range(n)], axis=0))
        steps = 2
        step = rows // steps

        def contracted(at):
            block = jnp.concatenate([visitor(d, c + k)[at, :] for k in range(n)], axis=1)
            v_high, v_low = split(block)
            value = dot3(v_high, v_low, t_high, t_low)
            return value if first else grad[at, :] + value

        if last:
            for r in range(steps):
                value = contracted(pl.ds(r * step, step))
                for k in range(chunks):
                    out[pl.ds(r * step * chunks + k, step, stride=chunks), :] = value[:, k * LANES:(k + 1) * LANES]
        else:

            @pl.loop(0, steps)
            def _(r):
                at = pl.ds(pl.multiple_of(r * step, step), step)
                grad[at, :] = contracted(at)

    def stage_z(c):
        x1(c).wait_recv()
        z_vis(c).start()

    def stage_v(c):
        w1(c).wait_recv()
        x2(c).start()

    def stage_x(c):
        for p in pieces_of(c):
            z_own(p).wait_recv()
        x3(c).start()

    def act(ops, middle):
        for op in ops:
            k = int(op[1:])
            if op[0] == "y":
                z_own(k).start()
            elif op[0] == "z":
                stage_z(k)
            elif op[0] == "v":
                stage_v(k)
            elif op[0] == "x":
                stage_x(k)
            else:
                {"B": stage_b, "C": stage_c, "D": stage_d}[op[0]](k, middle)

    kinds = [(side == 0) & is_end, (side == 0) & is_mid, (side == 1) & is_end, (side == 1) & is_mid]
    order = [common for _, common in PLAN if common[:1] == "E"]
    for by_kind, common in PLAN:
        for kind, ops in enumerate(by_kind):
            if ops:
                pl.when(kinds[kind])(lambda ops=ops, kind=kind: act(ops, kind % 2 == 1))
        if common[:1] == "A":
            stage_a(int(common[1:]))
        if common[:1] == "E":
            stage_e(int(common[1:]), common == order[0], common == order[-1])

    for c in range(chunks):
        for copy in (x2, x3, w1):
            copy(c).wait_send()
    for p in range(len(PIECES)):
        x1(p).wait_send()
        z_own(p).wait_send()
    for u in range(len(UNITS)):
        c1(u).wait_send()
        c2(u).wait_send()

        @pl.when(is_end)
        def _():
            e(u).wait_send()

        @pl.when(is_mid)
        def _():
            m(u).wait_send()
            t(u).wait_send()


def write_out(source, result, done):
    step = source.shape[0] // done.shape[0]
    copies = []
    for k in range(done.shape[0]):
        at = pl.ds(k * step, step)
        copies.append(pltpu.make_async_copy(source.at[at], result.at[at], done.at[k]))
    for copy in copies:
        copy.start()
    for copy in copies:
        copy.wait()


def on_device(factors, eps_occ, eps_virt, pair_mask):
    rows, _, width = factors.shape
    chunks = width // LANES
    zl = lax.axis_size("aux") // 2
    n_q = lax.axis_size("occ") // 2
    units, hw = len(UNITS), width // 2
    pairs = OFFSETS + 1
    dma = pltpu.SemaphoreType.DMA
    vmem = pltpu.VMEM
    sizes = (rows, width, chunks, zl, 4, n_q)
    in_vmem = pl.BlockSpec(memory_space=pltpu.VMEM)
    in_smem = pl.BlockSpec(memory_space=pltpu.SMEM)
    grad = pl.pallas_call(
        lambda *refs: kernel(sizes, *refs),
        name="ri_mp2",
        out_shape=jax.ShapeDtypeStruct((rows * chunks, LANES), F32),
        in_specs=[in_vmem, in_vmem, in_smem, in_smem],
        out_specs=in_vmem,
        scratch_shapes=[
            vmem((chunks, rows + PAD, LANES), F32),
            vmem((rows, width), F32),
            vmem((OFFSETS, chunks, rows + PAD, LANES), F32),
            vmem((width, rows), BF16),
            vmem((width, rows), BF16),
            vmem((width, LANES), F32),
            vmem((pairs, chunks, width, LANES), F32),
            vmem((pairs, chunks, hw, LANES), F32),
            vmem((pairs, chunks, hw, LANES), F32),
            vmem((pairs, chunks, hw, LANES), F32),
            vmem((pairs, chunks, hw, LANES), F32),
            vmem((pairs, chunks, hw, LANES), F32),
            vmem((pairs, chunks, width, LANES), F32),
            vmem((chunks, rows + PAD, LANES), F32),
        ]
        + [dma((len(PIECES),))] * 10
        + [dma((units,))] * 10,
        compiler_params=pltpu.CompilerParams(
            collective_id=0, has_side_effects=True, vmem_limit_bytes=VMEM_MIB * 1024 * 1024
        ),
    )(factors.reshape(rows * chunks, LANES), eps_virt.reshape(chunks, LANES), eps_occ, pair_mask)
    result = pl.pallas_call(
        write_out,
        name="write_out",
        out_shape=jax.ShapeDtypeStruct(grad.shape, F32),
        in_specs=[pl.BlockSpec(memory_space=pl.ANY)],
        out_specs=pl.BlockSpec(memory_space=pltpu.HBM),
        scratch_shapes=[dma((8,))],
        compiler_params=pltpu.CompilerParams(vmem_limit_bytes=1024 * 1024),
    )(grad)
    return result.reshape(factors.shape)


def solution(mesh):
    in_specs = (P("aux", "occ", None), P("occ"), P(), P("occ", None))
    out_specs = P("aux", "occ", None)
    return jax.shard_map(
        on_device, mesh=mesh, in_specs=in_specs, out_specs=out_specs, check_vma=False
    )
```

```python
import jax
import jax.numpy as jnp
from jax import lax
from jax.experimental import pallas as pl
from jax.experimental.pallas import tpu as pltpu
from jax.sharding import PartitionSpec as P

OFFSETS = 4
LANES = 128
PAD = 8
VMEM_MIB = 48
MESH = pl.DeviceIdType.MESH
F32 = jnp.float32
BF16 = jnp.bfloat16

UNITS = [(0, 0, 1, 0, 128), (0, 1, 1, 0, 256), (0, 2, 1, 0, 384), (0, 3, 1, 0, 512), (2, 0, 1, 0, 512), (2, 1, 1, 0, 512), (2, 2, 1, 0, 256), (2, 2, 1, 256, 512), (2, 3, 1, 0, 256), (2, 3, 1, 256, 512), (4, 0, 1, 0, 512), (4, 1, 1, 0, 512), (4, 2, 1, 0, 256), (4, 2, 1, 256, 512), (4, 3, 1, 0, 256), (4, 3, 1, 256, 512), (1, 0, 2, 0, 512), (1, 2, 1, 0, 512), (1, 3, 1, 0, 512), (3, 0, 1, 0, 512), (3, 1, 1, 0, 512), (3, 2, 1, 0, 512), (3, 3, 1, 0, 256), (3, 3, 1, 256, 512)]
EARLY = 10
PLAN = [
    ([[], [], [], []], 'A3'),
    ([[], [], ['z0'], ['z0']], 'A1'),
    ([[], [], [], []], 'A2'),
    ([[], [], ['z1'], ['z1']], 'A0'),
    ([['B2', 'B0'], ['B2', 'B0'], ['B0', 'z2', 'z3'], ['B0', 'z2', 'C0', 'z3']], 'A4'),
    ([['v0'], ['v0'], ['v0', 'z4', 'z5'], ['v0', 'D0', 'z4', 'z5']], 'A5'),
    ([['v1', 'x0'], ['v1', 'x0'], ['v1', 'x0', 'D0', 'z6', 'z7'], ['v1', 'x0', 'z6', 'z7']], 'A6'),
    ([['v2'], ['v2'], ['v2'], ['v2']], 'A7'),
    ([[], [], ['z8', 'z9'], ['z8', 'z9']], 'A8'),
    ([['v3'], ['v3'], ['v3'], ['v3']], 'A9'),
    ([['x1'], ['x1'], ['x1'], ['x1']], 'A16'),
    ([['B16'], ['B16'], ['B16'], ['B16']], 'A19'),
    ([[], [], [], []], 'A10'),
    ([['B19'], ['B19'], ['B19'], ['B19']], 'A20'),
    ([[], [], [], []], 'A11'),
    ([['B20', 'B11', 'x2', 'B3', 'B1'], ['B20', 'B11', 'x2', 'B3', 'B1'], ['x2', 'B3', 'B1', 'B2', 'B20'], ['B20', 'x2', 'B3', 'B1', 'B2']], 'A17'),
    ([['B17'], ['B17'], ['B11', 'B17'], ['B11', 'B17']], 'A12'),
    ([[], [], [], []], 'A13'),
    ([[], [], ['B12', 'B13'], ['B12', 'B13']], 'A21'),
    ([['B21'], ['B21'], ['B21'], ['B21']], 'A14'),
    ([[], [], [], []], 'A15'),
    ([['x3', 'B6', 'B7', 'B12', 'B13', 'B10', 'B5', 'B8', 'B9', 'B4', 'B14', 'B15'], ['C2', 'C0', 'x3', 'B6', 'B7', 'B12', 'B13', 'B10', 'B5', 'B8', 'B9', 'B4', 'B14', 'B15'], ['x3', 'B6', 'B7', 'B10', 'B5', 'B8', 'B9', 'B4', 'B14', 'B15'], ['x3', 'B6', 'B7', 'B10', 'B5', 'B8', 'B9', 'B4', 'B14', 'B15']], 'A18'),
    ([['B18', 'D2', 'D0'], ['D2', 'D0', 'B18', 'C16', 'C19', 'C20', 'D16', 'C11'], ['B18'], ['B18', 'C16', 'C19']], 'A22'),
    ([[], [], [], ['C3']], 'A23'),
    ([['B22', 'B23', 'D16'], [], ['B22', 'B23', 'D16'], ['B22', 'C1', 'D16', 'B23', 'C2']], 'E16'),
    ([['D19'], ['D19', 'C3', 'B22', 'B23', 'C1', 'D20'], ['D19'], ['D19', 'C20', 'D3']], 'E19'),
    ([['D20'], [], ['D3', 'D1', 'D2', 'D20'], ['D1', 'C11', 'D2', 'C17', 'D20', 'C12', 'C13', 'D11']], 'E20'),
    ([['D11', 'D3', 'D1'], ['D11', 'C17', 'D3', 'C21', 'C6', 'D1', 'C7'], [], []], 'E3'),
    ([[], [], ['D11'], ['C21']], 'E11'),
    ([['D17'], ['D17', 'C12', 'C13'], ['D17', 'D12'], ['D17', 'C6', 'C7', 'D12']], 'E17'),
    ([['D21', 'D6'], ['D21', 'D6', 'C10', 'D7'], ['D13', 'D21', 'D6'], ['D13', 'C10', 'D21', 'C5', 'D6']], 'E21'),
    ([['D7', 'D12', 'D13'], ['D12', 'C5', 'D13', 'C8', 'C9'], [], []], 'E13'),
    ([[], [], ['D7'], ['D7', 'C8', 'C9']], 'E7'),
    ([['D10'], ['D10', 'C4'], ['D10'], ['D10', 'C4']], 'E10'),
    ([['D5', 'D8'], ['D5', 'C14', 'C15', 'D8'], ['D5', 'D8'], ['D5', 'C14', 'C15', 'D8']], 'E5'),
    ([['D9'], ['D9', 'C18'], ['D9'], ['D9', 'C18']], 'E9'),
    ([['D4', 'D14'], ['D4', 'C22', 'C23', 'D14'], ['D4', 'D14'], ['D4', 'C22', 'C23', 'D14']], 'E4'),
    ([['D15'], ['D15'], ['D15'], ['D15']], 'E15'),
    ([['D18', 'D22'], ['D18', 'D22'], ['D18', 'D22'], ['D18', 'D22']], 'E18'),
    ([['D23'], ['D23'], ['D23'], ['D23']], 'E23'),
]

PIECES = [(0, 0, 128), (0, 128, 128), (0, 256, 256), (0, 512, 512 + PAD), (1, 0, 512), (1, 512, 512), (2, 0, 512), (2, 512, 512), (3, 0, 512), (3, 512, 512)]


def split(value):
    high = value.astype(BF16)
    return high, (value - high.astype(F32)).astype(BF16)


def dot3(a_high, a_low, b_high, b_low):
    def one(a, b):
        return lax.dot_general(a, b, (((1,), (0,)), ((), ())), preferred_element_type=F32)

    return one(a_high, b_high) + (one(a_high, b_low) + one(a_low, b_high))


def kernel(sizes, factors, eps_virt, eps_occ, mask, out, own, grad, vis, own_th, own_tl, row_e, part, core_in, half, end_in, mid, mid_in, amp, via, *sems):
    rows, width, chunks, zl, n_x, n_q = sizes
    (ws, wr, x1s, x1r, x2s, x2r, zs, zr, x3s, x3r, c1s, c1r, es, er, ms, mr, ts, tr, c2s, c2r) = sems
    hw = width // 2
    aux, occ = lax.axis_index("aux"), lax.axis_index("occ")
    core, z_lo = lax.rem(aux, 2), aux // 2
    side, q = lax.rem(occ, 2), occ // 2

    def along(k):
        return (aux, lax.rem(q + k + n_q, n_q) * 2 + side)

    def at_z(z):
        return (z * 2 + core, occ)

    across = (aux, q * 2 + 1 - side)
    partner = (z_lo * 2 + 1 - core, occ)
    low_half = z_lo < zl // 2
    is_mid = (z_lo == zl // 2 - 1) | (z_lo == zl // 2)
    is_end = jnp.logical_not(is_mid)
    mid_of_end = jnp.where(low_half, 1, zl - 2)
    end_of_mid = jnp.where(low_half, 0, zl - 1)
    other_mid = jnp.where(low_half, zl - 2, 1)

    def rows_of(u):
        return UNITS[u][4] - UNITS[u][3]

    def share(u, which):
        size = rows_of(u) // 2
        return pl.ds(pl.multiple_of(UNITS[u][3] + which * size, size), size)

    def mine(u):
        return share(u, core)

    def theirs(u):
        return share(u, 1 - core)

    def first_rows(u):
        return pl.ds(UNITS[u][3] // 2, rows_of(u) // 2)

    def in_row(k, step):
        at = lax.rem(k + n_q, n_q)
        x_at = lax.rem(at, n_x)
        return (aux, (at - x_at + lax.rem(x_at + step, n_x)) * 2 + side)

    x2_from = in_row(q, 1)
    before = q - lax.rem(q, n_x) + lax.rem(lax.rem(q, n_x) + n_x - 1, n_x)
    w1_from = (aux, lax.rem(before - 2 + n_q, n_q) * 2 + side)

    barrier = pltpu.get_barrier_semaphore()

    def tell(device):
        pl.semaphore_signal(barrier, inc=1, device_id=device, device_id_type=MESH)

    for device in (along(-1), x2_from, w1_from, across, partner):
        tell(device)

    @pl.when(is_mid)
    def _():
        tell(at_z(end_of_mid))
        tell(at_z(other_mid))

    @pl.when(is_end)
    def _():
        tell(at_z(mid_of_end))

    eps = jnp.full((1, LANES), eps_occ[0], F32)
    live = [
        jnp.full((1, LANES), jnp.where(occ >= d, mask[0, d - 1], 0), jnp.int32).astype(F32)
        for d in range(1, OFFSETS + 1)
    ]
    blank = jnp.zeros((PAD - 2 - OFFSETS, LANES), F32)
    for c in range(chunks):
        own[c, pl.ds(0, rows), :] = factors[pl.ds(c, rows, stride=chunks), :]
        own[c, pl.ds(rows, PAD), :] = jnp.concatenate([eps, eps_virt[pl.ds(c, 1), :], *live, blank], axis=0)

    @pl.when(is_mid)
    def _():
        pl.semaphore_wait(barrier, 7)

    @pl.when(is_end)
    def _():
        pl.semaphore_wait(barrier, 6)

    def remote(src, dst, send, recv, device):
        return pltpu.make_async_remote_copy(src, dst, send, recv, device_id=device, device_id_type=MESH)

    def full(c):
        return pl.ds(0, rows + PAD if c == 0 else rows)

    def piece(ref, p, *slot):
        c, row, size = PIECES[p]
        return ref.at[(*slot, c, pl.ds(row, size))]

    def pieces_of(c):
        return [p for p, item in enumerate(PIECES) if item[0] == c]

    def x1(p):
        return remote(piece(own, p), piece(vis, p, 1), x1s.at[p], x1r.at[p], along(1))

    def w1(c):
        return remote(own.at[c, full(c)], via.at[c, full(c)], ws.at[c], wr.at[c], in_row(q + 2, 1))

    def x2(c):
        return remote(via.at[c, full(c)], vis.at[3, c, full(c)], x2s.at[c], x2r.at[c], in_row(q, n_x - 1))

    def z_own(p):
        return remote(piece(own, p), piece(vis, p, 0), zs.at[p], zr.at[p], across)

    def z_vis(p):
        return remote(piece(vis, p, 1), piece(vis, p, 0), zs.at[p], zr.at[p], across)

    def x3(c):
        return remote(vis.at[0, c, full(c)], vis.at[2, c, full(c)], x3s.at[c], x3r.at[c], along(1))

    def first_hop(p):
        x1(p).start()
        if p < EARLY:

            @pl.when(side == 0)
            def _():
                z_own(p).start()

    for p in range(len(PIECES)):
        if p == 4:
            w1(0).start()
        first_hop(p)
    for c in range(1, chunks):
        w1(c).start()

    for c in range(chunks):
        high, low = split(own[c, :rows, :].T)
        own_th[pl.ds(c * LANES, LANES), :] = high
        own_tl[pl.ds(c * LANES, LANES), :] = low
        virt = own[c, pl.ds(rows + 1, 1), :]
        eps = own[c, pl.ds(rows, 1), :]
        row_e[pl.ds(c * LANES, LANES), :] = jnp.broadcast_to(virt - eps, (LANES, LANES)).T

    def visitor(d, c):
        return own.at[c] if d == 0 else vis.at[d - 1, c]

    def c1(u):
        d, c, n = UNITS[u][:3]
        at = pl.ds(c, n)
        return remote(part.at[d, at, theirs(u)], core_in.at[d, at, first_rows(u)], c1s.at[u], c1r.at[u], partner)

    def e(u):
        d, c, n = UNITS[u][:3]
        at = pl.ds(c, n)
        return remote(half.at[d, at, first_rows(u)], end_in.at[d, at, first_rows(u)], es.at[u], er.at[u], at_z(mid_of_end))

    def m(u):
        d, c, n = UNITS[u][:3]
        at = pl.ds(c, n)
        return remote(mid.at[d, at, first_rows(u)], mid_in.at[d, at, first_rows(u)], ms.at[u], mr.at[u], at_z(other_mid))

    def t(u):
        d, c, n = UNITS[u][:3]
        block = amp.at[d, pl.ds(c, n), mine(u)]
        return remote(block, block, ts.at[u], tr.at[u], at_z(end_of_mid))

    def c2(u):
        d, c, n = UNITS[u][:3]
        block = amp.at[d, pl.ds(c, n), mine(u)]
        return remote(block, block, c2s.at[u], c2r.at[u], partner)

    def joined(d, c, n):
        return jnp.concatenate([visitor(d, c + k)[:rows, :] for k in range(n)], axis=1)

    arrived = set()

    def stage_a(u):
        d, c, n = UNITS[u][:3]
        for k in range(c, c + n):
            if (d, k) in arrived:
                continue
            arrived.add((d, k))
            if d == 3:
                x3(k).wait_recv()
            if d == 4:
                x2(k).wait_recv()
            if d == 2:

                @pl.when(side == 0)
                def _():
                    for p in pieces_of(k):
                        x1(p).wait_recv()

        v_high, v_low = split(joined(d, c, n))

        at = pl.ds(UNITS[u][3], rows_of(u))
        value = dot3(own_th[at, :], own_tl[at, :], v_high, v_low)
        for k in range(n):
            part[d, c + k, at, :] = value[:, k * LANES:(k + 1) * LANES]
        c1(u).start()

    def stage_b(u, middle):
        d, c, n = UNITS[u][:3]
        c1(u).wait_recv()
        for k in range(n):
            half[d, c + k, first_rows(u), :] = part[d, c + k, mine(u), :] + core_in[d, c + k, first_rows(u), :]
        if not middle:
            e(u).start()

    def stage_c(u, middle):
        d, c, n = UNITS[u][:3]
        if middle:
            e(u).wait_recv()
            for k in range(n):
                mid[d, c + k, first_rows(u), :] = half[d, c + k, first_rows(u), :] + end_in[d, c + k, first_rows(u), :]
            m(u).start()

    def stage_d(u, middle):
        d, c, n = UNITS[u][:3]
        if middle:
            m(u).wait_recv()
            for k in range(n):
                total = mid[d, c + k, first_rows(u), :] + mid_in[d, c + k, first_rows(u), :]
                virt = own[c + k, pl.ds(rows + 1, 1), :]
                eps = visitor(d, 0)[pl.ds(rows, 1), :]
                value = -total / (row_e[mine(u), :] + (virt - eps))
                if d > 0:
                    live = own[c + k, pl.ds(rows + 1 + d, 1), :]
                    value = jnp.where(live > 0, value, jnp.zeros_like(value))
                amp[d, c + k, mine(u), :] = value
            t(u).start()
        else:
            t(u).wait_recv()
        c2(u).start()

    def transposed(d, c):
        if d > 0:
            return amp[d, c].T
        blocks = [
            amp[0, c, pl.ds(r * LANES, LANES), :].T if r <= c else amp[0, r, pl.ds(c * LANES, LANES), :]
            for r in range(chunks)
        ]
        return jnp.concatenate(blocks, axis=1)

    def stage_e(u, first, last):
        d, c, n = UNITS[u][:3]
        for k, other in enumerate(UNITS):
            if other[0] == d and (d == 0 or other[1] == c):
                c2(k).wait_recv()
        if d == 0:
            c, n = 0, chunks
        t_high, t_low = split(jnp.concatenate([transposed(d, c + k) for k in range(n)], axis=0))
        steps = 2
        step = rows // steps

        def contracted(at):
            block = jnp.concatenate([visitor(d, c + k)[at, :] for k in range(n)], axis=1)
            v_high, v_low = split(block)
            value = dot3(v_high, v_low, t_high, t_low)
            return value if first else grad[at, :] + value

        if last:
            for r in range(steps):
                value = contracted(pl.ds(r * step, step))
                for k in range(chunks):
                    out[pl.ds(r * step * chunks + k, step, stride=chunks), :] = value[:, k * LANES:(k + 1) * LANES]
        else:

            @pl.loop(0, steps)
            def _(r):
                at = pl.ds(pl.multiple_of(r * step, step), step)
                grad[at, :] = contracted(at)

    def stage_z(c):
        x1(c).wait_recv()
        z_vis(c).start()

    def stage_v(c):
        w1(c).wait_recv()
        x2(c).start()

    def stage_x(c):
        for p in pieces_of(c):
            z_own(p).wait_recv()
        x3(c).start()

    def act(ops, middle):
        for op in ops:
            k = int(op[1:])
            if op[0] == "y":
                z_own(k).start()
            elif op[0] == "z":
                stage_z(k)
            elif op[0] == "v":
                stage_v(k)
            elif op[0] == "x":
                stage_x(k)
            else:
                {"B": stage_b, "C": stage_c, "D": stage_d}[op[0]](k, middle)

    kinds = [(side == 0) & is_end, (side == 0) & is_mid, (side == 1) & is_end, (side == 1) & is_mid]
    order = [common for _, common in PLAN if common[:1] == "E"]
    for by_kind, common in PLAN:
        for kind, ops in enumerate(by_kind):
            if ops:
                pl.when(kinds[kind])(lambda ops=ops, kind=kind: act(ops, kind % 2 == 1))
        if common[:1] == "A":
            stage_a(int(common[1:]))
        if common[:1] == "E":
            stage_e(int(common[1:]), common == order[0], common == order[-1])

    for c in range(chunks):
        for copy in (x2, x3, w1):
            copy(c).wait_send()
    for p in range(len(PIECES)):
        x1(p).wait_send()
        z_own(p).wait_send()
    for u in range(len(UNITS)):
        c1(u).wait_send()
        c2(u).wait_send()

        @pl.when(is_end)
        def _():
            e(u).wait_send()

        @pl.when(is_mid)
        def _():
            m(u).wait_send()
            t(u).wait_send()


def write_out(source, result, done):
    step = source.shape[0] // done.shape[0]
    copies = []
    for k in range(done.shape[0]):
        at = pl.ds(k * step, step)
        copies.append(pltpu.make_async_copy(source.at[at], result.at[at], done.at[k]))
    for copy in copies:
        copy.start()
    for copy in copies:
        copy.wait()


def on_device(factors, eps_occ, eps_virt, pair_mask):
    rows, _, width = factors.shape
    chunks = width // LANES
    zl = lax.axis_size("aux") // 2
    n_q = lax.axis_size("occ") // 2
    units, hw = len(UNITS), width // 2
    pairs = OFFSETS + 1
    dma = pltpu.SemaphoreType.DMA
    vmem = pltpu.VMEM
    sizes = (rows, width, chunks, zl, 4, n_q)
    in_vmem = pl.BlockSpec(memory_space=pltpu.VMEM)
    in_smem = pl.BlockSpec(memory_space=pltpu.SMEM)
    grad = pl.pallas_call(
        lambda *refs: kernel(sizes, *refs),
        name="ri_mp2",
        out_shape=jax.ShapeDtypeStruct((rows * chunks, LANES), F32),
        in_specs=[in_vmem, in_vmem, in_smem, in_smem],
        out_specs=in_vmem,
        scratch_shapes=[
            vmem((chunks, rows + PAD, LANES), F32),
            vmem((rows, width), F32),
            vmem((OFFSETS, chunks, rows + PAD, LANES), F32),
            vmem((width, rows), BF16),
            vmem((width, rows), BF16),
            vmem((width, LANES), F32),
            vmem((pairs, chunks, width, LANES), F32),
            vmem((pairs, chunks, hw, LANES), F32),
            vmem((pairs, chunks, hw, LANES), F32),
            vmem((pairs, chunks, hw, LANES), F32),
            vmem((pairs, chunks, hw, LANES), F32),
            vmem((pairs, chunks, hw, LANES), F32),
            vmem((pairs, chunks, width, LANES), F32),
            vmem((chunks, rows + PAD, LANES), F32),
        ]
        + [dma((len(PIECES),))] * 10
        + [dma((units,))] * 10,
        compiler_params=pltpu.CompilerParams(
            collective_id=0, has_side_effects=True, vmem_limit_bytes=VMEM_MIB * 1024 * 1024
        ),
    )(factors.reshape(rows * chunks, LANES), eps_virt.reshape(chunks, LANES), eps_occ, pair_mask)
    result = pl.pallas_call(
        write_out,
        name="write_out",
        out_shape=jax.ShapeDtypeStruct(grad.shape, F32),
        in_specs=[pl.BlockSpec(memory_space=pl.ANY)],
        out_specs=pl.BlockSpec(memory_space=pltpu.HBM),
        scratch_shapes=[dma((8,))],
        compiler_params=pltpu.CompilerParams(vmem_limit_bytes=1024 * 1024),
    )(grad)
    return result.reshape(factors.shape)


def solution(mesh):
    in_specs = (P("aux", "occ", None), P("occ"), P(), P("occ", None))
    out_specs = P("aux", "occ", None)
    return jax.shard_map(
        on_device, mesh=mesh, in_specs=in_specs, out_specs=out_specs, check_vma=False
    )
```
